512 devices in a mesh: seq: 128 (over z, y, core), head: 4 (over x).
Axes of the slice: x: 4, y: 4, z: 16, core: 2. Of those that a mesh axis runs over, the one named last changes fastest.
Arguments:
- query_states: float32 [32768, 2048], P('seq', 'head'), may hold values from -6.4 to 6.4
- key_states: float32 [32768, 2048], P('seq', 'head'), may hold values from -6.4 to 6.4
- value_states: float32 [32768, 2048], P('seq', 'head'), may hold values from -30 to 30
- out_cotangent: float32 [32768, 2048], P('seq', 'head'), may hold values from -20 to 20
- norm_gain: float32 [2048], P('head'), may hold values from 0.5 to 1.5
- norm_bias: float32 [2048], P('head'), may hold values from -3 to 3
Outputs:
- normed: float32 [32768, 2048], P('seq', 'head')
- query_grad: float32 [32768, 2048], P('seq', 'head')
- key_grad: float32 [32768, 2048], P('seq', 'head')
- value_grad: float32 [32768, 2048], P('seq', 'head')
The draws below stay inside these ranges and needn't reach their ends.
All inputs are finite; a program needn't handle non-finite values.
Results may differ from the reference program's by a relative error of at most 0.0003.
Values sent between devices are 32-bit elements; how exact they have to be, the bound alone decides.
No kernel may reach another device: no remote copies, remote signals or barrier semaphores. Data moves between devices by JAX's collectives and lax.ppermute only.
A program may use at most 64 MiB of HBM per device.

```python
import math
import jax
import jax.numpy as jnp
from jax import lax

D = 2048
HEADS = 16
BLK = 128
LEV = 5
SEQ = 32768


def draw_pair(key):
    full_shape = (SEQ, D)
    base_query = jax.random.normal(jax.random.fold_in(key, 11), full_shape, jnp.float32)
    base_key = jax.random.normal(jax.random.fold_in(key, 12), full_shape, jnp.float32)
    query_draw = jnp.clip(1.6 * base_query, -6.4, 6.4)
    key_draw = jnp.clip(1.6 * base_key, -6.4, 6.4)
    return (query_draw, key_draw)


def draw_query_states(key, part):
    return draw_pair(key)[0]


def draw_key_states(key, part):
    return draw_pair(key)[1]


def draw_value_states(key, part):
    full_shape = (SEQ, D)
    column = jnp.arange(D).astype(jnp.float32)
    column_scale = 0.5 * jnp.exp(math.log(3.0) * column / (D - 1)) * jnp.exp(jax.random.uniform(jax.random.fold_in(key, 22), (D,), jnp.float32, 0.0, math.log(4.0)))
    row_scale = jnp.exp(jax.random.uniform(jax.random.fold_in(key, 23), (SEQ,), jnp.float32, 0.0, math.log(10.0))) / 3.0
    noise_draw = jax.random.normal(jax.random.fold_in(key, 21), full_shape, jnp.float32)
    segment = jnp.repeat(jax.random.normal(jax.random.fold_in(key, 24), (SEQ // 64, D), jnp.float32), 64, axis=0)
    drawn = (noise_draw * row_scale[:, None] + segment) * column_scale[None, :]
    return jnp.clip(drawn, -30.0, 30.0)


def draw_out_cotangent(key, part):
    full_shape = (SEQ, D)
    column = jnp.arange(D).astype(jnp.float32)
    column_scale = jnp.exp(math.log(3.0) * column / (D - 1)) * jnp.exp(jax.random.uniform(jax.random.fold_in(key, 32), (D,), jnp.float32, 0.0, math.log(3.0)))
    noise_draw = jax.random.normal(jax.random.fold_in(key, 31), full_shape, jnp.float32)
    return jnp.clip(noise_draw * column_scale[None, :], -20.0, 20.0)


def level_of(key, dims, shards, smallest, top_value):
    def one(axis_at, parts):
        heights = jax.random.uniform(jax.random.fold_in(jax.random.fold_in(key, 6), axis_at), (parts,), jnp.float32, smallest / len(shards), top_value / len(shards))
        return jnp.repeat(jnp.exp(heights), dims[axis_at] // parts).reshape((-1,) + (1,) * (len(dims) - axis_at - 1))

    loudness = one(*shards[0])
    for cut in shards[1:]:
        loudness = loudness * one(*cut)
    return loudness


def bell_draw(rng, dims, spread, most, split=(), held_as=jnp.bfloat16):
    loudness = level_of(rng, dims, split, -0.22, 0.18) if split else 1.0
    result = jax.random.normal(rng, dims, jnp.float32) * spread * loudness
    return jnp.minimum(jnp.maximum(result, -most), most).astype(held_as)


def setup_inputs(seed: int = 0) -> dict:
    arg_keys = jax.random.split(jax.random.key(seed), 7)
    query_states = draw_query_states(jax.random.fold_in(arg_keys[6], 71), 0)
    key_states = draw_key_states(jax.random.fold_in(arg_keys[6], 71), 0)
    value_states = draw_value_states(jax.random.fold_in(arg_keys[6], 71), 0)
    out_cotangent = draw_out_cotangent(jax.random.fold_in(arg_keys[6], 71), 0)
    norm_gain = jnp.clip(1.0 + 0.1 * jax.random.normal(arg_keys[4], (D,), jnp.float32), 0.5, 1.5)
    norm_bias = bell_draw(arg_keys[5], (D,), 0.5, 3.0, ((0, 4),), jnp.float32)
    return {"query_states": query_states, "key_states": key_states, "value_states": value_states, "out_cotangent": out_cotangent, "norm_gain": norm_gain, "norm_bias": norm_bias}


FULL_PRECISION = lax.Precision.HIGHEST
NORM_EPSILON = 1e-05

def levels_used(seq_total):
    deepest = 0
    for height in range(1, LEV + 1):
        if BLK * 2 ** (height + 1) <= seq_total:
            deepest = height
    return deepest

def coarsen(stacked, factor):
    return stacked.reshape((stacked.shape[0] // factor, factor) + stacked.shape[1:]).mean(axis=1)

def sibling_blocks(stacked):
    grouped = stacked.reshape((stacked.shape[0] // (2 * BLK), 2, BLK) + stacked.shape[1:])
    return jnp.flip(grouped, axis=1).reshape((stacked.shape[0] // BLK, BLK) + stacked.shape[1:])

def head_attention(triple):
    query_rows, key_rows, value_rows = triple
    head_dim = D // HEADS
    inv_root = 1.0 / math.sqrt(head_dim)
    near_groups = SEQ // (2 * BLK)
    near_scores = jnp.einsum('nqd,nkd->nqk', query_rows.reshape(near_groups, 2 * BLK, head_dim), key_rows.reshape(near_groups, 2 * BLK, head_dim), precision=FULL_PRECISION) * inv_root
    score_list = [near_scores.reshape(SEQ, 2 * BLK)]
    weight_list = [jnp.ones((2 * BLK,), jnp.float32)]
    value_list = [value_rows.reshape(near_groups, 2 * BLK, head_dim)]
    for height in range(1, levels_used(SEQ) + 1):
        factor = 2 ** height
        groups = SEQ // (BLK * factor)
        sib_keys = sibling_blocks(coarsen(key_rows, factor))
        sib_values = sibling_blocks(coarsen(value_rows, factor))
        level_scores = jnp.einsum('nqd,nkd->nqk', query_rows.reshape(groups, BLK * factor, head_dim), sib_keys, precision=FULL_PRECISION) * inv_root
        score_list.append(level_scores.reshape(SEQ, BLK))
        weight_list.append(jnp.full((BLK,), float(factor), jnp.float32))
        value_list.append(sib_values)
    all_scores = jnp.concatenate(score_list, axis=1)
    row_max = lax.stop_gradient(lax.optimization_barrier(jnp.max(all_scores, axis=1, keepdims=True)))
    weighted = jnp.exp(all_scores - row_max) * jnp.concatenate(weight_list)[None, :]
    denominator = lax.optimization_barrier(jnp.sum(weighted, axis=1, keepdims=True))
    numerator = jnp.zeros((SEQ, head_dim), jnp.float32)
    offset = 0
    for value_blocks in value_list:
        width_here = value_blocks.shape[1]
        groups = value_blocks.shape[0]
        level_weights = weighted[:, offset:offset + width_here].reshape(groups, SEQ // groups, width_here)
        numerator = numerator + jnp.einsum('nqk,nkd->nqd', level_weights, value_blocks, precision=FULL_PRECISION).reshape(SEQ, head_dim)
        offset = offset + width_here
    return numerator / denominator

def reference(query_states, key_states, value_states, out_cotangent, norm_gain, norm_bias):
    head_dim = D // HEADS

    def to_heads(matrix):
        return matrix.reshape(SEQ, HEADS, head_dim).transpose(1, 0, 2)

    def forward(query_all, key_all, value_all):
        per_head = lax.map(jax.checkpoint(head_attention), (to_heads(query_all), to_heads(key_all), to_heads(value_all)))
        attended = per_head.transpose(1, 0, 2).reshape(SEQ, D)
        mean_row = lax.optimization_barrier(jnp.mean(attended, axis=1, keepdims=True))
        centered = attended - mean_row
        variance = lax.optimization_barrier(jnp.mean(centered * centered, axis=1, keepdims=True))
        return centered * lax.rsqrt(variance + NORM_EPSILON) * norm_gain[None, :] + norm_bias[None, :]
    normed, pullback = jax.vjp(forward, query_states, key_states, value_states)
    query_grad, key_grad, value_grad = pullback(out_cotangent)
    return (normed, query_grad, key_grad, value_grad)
```

```python
import functools
import math

import jax
import jax.numpy as jnp
from jax import lax
from jax.experimental import pallas as pl
from jax.experimental.pallas import tpu as pltpu
from jax.sharding import PartitionSpec as P

D = 2048
HEADS = 16
BLK = 128
EPS = 1e-05
HD = D // HEADS
INV_ROOT = 1.0 / math.sqrt(HD)
LOG2E = 1.0 / math.log(2.0)

L45 = ((16, 4), (16, 5))
GATHERED = ((64, 2),) + L45 + ((32, 3),) + L45 + ((32, 3),) + L45 + L45
NEAR = 256
OWN = 256
PEER = 384
KEYS = NEAR + OWN + PEER
LEVELS = ((NEAR, 0),) + GATHERED + ((128, 1),) + GATHERED

VM = pl.BlockSpec(memory_space=pltpu.VMEM)
SM = pl.BlockSpec(memory_space=pltpu.SMEM)
F32 = jnp.float32
BF16 = jnp.bfloat16


def shape(*dims):
    return jax.ShapeDtypeStruct(dims, F32)


def call(body, out, args, name, scalars=0, scratch=()):
    return pl.pallas_call(
        body,
        out_shape=out,
        in_specs=[SM] * scalars + [VM] * (len(args) - scalars),
        out_specs=jax.tree.map(lambda _: VM, out),
        scratch_shapes=scratch,
        name=name,
    )(*args)


def halves(value, buf):
    rows = value.shape[0] // 2
    buf[...] = value
    return 0.5 * (buf[pl.ds(0, rows, stride=2), :] + buf[pl.ds(1, rows, stride=2), :])


def doubled(value, buf):
    rows = value.shape[0]
    half = 0.5 * value
    buf[pl.ds(0, rows, stride=2), :] = half
    buf[pl.ds(1, rows, stride=2), :] = half
    return buf[...]


def buffers(count, *rows):
    return [pltpu.VMEM((count, n, HD), F32) for n in rows]


def coarsen_body(k_ref, v_ref, l1, l2, l3, l4, b0, b1, b2, b3):
    for h in range(8):
        src = k_ref if h < 4 else v_ref
        col = slice((h % 4) * HD, (h % 4 + 1) * HD)
        to = slice(h * HD, (h + 1) * HD)
        one = halves(src[:, col], b0.at[h])
        l1[:, to] = one
        two = halves(one, b1.at[h])
        l2[:, to] = two
        three = halves(two, b2.at[h])
        l3[:, to] = three
        four = halves(three, b3.at[h])
        for j in range(4):
            l4[j, :, to] = four


def route_body(zpos, z_in, l3, c0, y23, buf):
    z = zpos[0]
    c0[0:16, :] = z_in[z ^ 1]
    for h in range(8):
        to = slice(h * HD, (h + 1) * HD)
        for j in (2, 3):
            c0[8 * j : 8 * j + 8, to] = halves(z_in[z ^ j, :, to], buf.at[2 * h + j - 2])
    y23[0:32, :] = l3[...]
    y23[32:64, :] = c0[...]


def pack_body(*refs):
    out = refs[-1]
    row = 0
    for ref in refs[:-1]:
        out[row : row + ref.shape[0], :] = ref[...]
        row += ref.shape[0]


def split2(x):
    hi = x.astype(BF16)
    return hi, (x - hi.astype(F32)).astype(BF16)


def split3(x):
    hi = x.astype(BF16)
    rest = x - hi.astype(F32)
    mid = rest.astype(BF16)
    return hi, mid, (rest - mid.astype(F32)).astype(BF16)


NT = (((1,), (1,)), ((), ()))
NN = (((1,), (0,)), ((), ()))
TN = (((0,), (0,)), ((), ()))


def dot(a, b, dims):
    return lax.dot_general(a, b, dims, preferred_element_type=F32)


def cat(*parts):
    return jnp.concatenate(parts, axis=1)


def scores(keys, query):
    kh, km, kl = split3(keys)
    qh, qm, ql = split3(query)
    key2 = cat(kh, km)
    return dot(key2, cat(qh, qh), NT) + (dot(key2, cat(qm, qm), NT) + dot(cat(kh, kl), cat(ql, qh), NT))


def dot_nt(a, b):
    ah, al = split2(a)
    bh, bl = split2(b)
    return dot(cat(ah, al), cat(bh, bh), NT) + dot(ah, bl, NT)


def dot_nn(ah, al, b):
    bh, bl = split2(b)
    both = dot(ah, cat(bh, bl), NN)
    half = b.shape[1]
    return both[:, :half] + both[:, half:] + dot(al, bh, NN)


def dot_tn(a, bh, bl):
    ah, al = split2(a)
    return dot(ah, bh, TN) + (dot(ah, bl, TN) + dot(al, bh, TN))


def head_cols(h):
    return slice(h * HD, (h + 1) * HD)


def forward_body(q_ref, k_ref, v_ref, own, peer, ct, gain, p_out, att, send):
    for h in range(4):
        at = head_cols(h)
        query = q_ref[:, at] * (INV_ROOT * LOG2E)
        vat = head_cols(4 + h)
        blocks = (
            scores(k_ref[:, at], query),
            scores(own[128:384, at], query),
            scores(peer[:, at], query),
        )
        s = jnp.concatenate(blocks, axis=0)
        parts = []
        row = 0
        for rows, level in LEVELS:
            seg = s[row : row + rows]
            parts.append(seg + float(level) if level else seg)
            row += rows
        s = jnp.concatenate(parts, axis=0)
        top = jnp.max(s, axis=0, keepdims=True)
        e = jnp.exp2(s - top)
        p = e * (1.0 / jnp.sum(e, axis=0, keepdims=True))
        p_out[h] = p
        values = jnp.concatenate((v_ref[:, at], own[128:384, vat], peer[:, vat]), axis=0)
        ph, pl_ = split2(p)
        att[:, at] = dot_tn(values, ph, pl_).T
    a = att[...]
    width = 4 * HD
    total = jnp.sum(a, axis=1, keepdims=True)
    mean = total * (1.0 / width)
    away = a - mean
    sg = ct[...] * gain[...]
    lane = lax.broadcasted_iota(jnp.int32, (NEAR, HD), 1)
    stats = jnp.where(lane == 0, mean, 0.0)
    for j, value in (
        (1, jnp.sum(away * away, axis=1, keepdims=True)),
        (2, jnp.sum(sg, axis=1, keepdims=True)),
        (3, jnp.sum(sg * away, axis=1, keepdims=True)),
    ):
        stats = jnp.where(lane == j, value, stats)
    rows = stats.T[0:8]
    for j in range(4):
        send[j] = rows


def backward_body(
    q_ref, k_ref, v_ref, own, peer, ct, gain, bias, p_in, att, got,
    normed, dq, dk, dv, d_own, d_peer,
):
    stat = [got[j] for j in range(4)]
    mean = (stat[0][0:1] + stat[1][0:1] + stat[2][0:1] + stat[3][0:1]) * 0.25
    square = jnp.zeros_like(mean)
    total = jnp.zeros_like(mean)
    cross = jnp.zeros_like(mean)
    for part in stat:
        shift = part[0:1] - mean
        square = square + (part[1:2] + (4.0 * HD) * (shift * shift))
        total = total + part[2:3]
        cross = cross + (part[3:4] + part[2:3] * shift)
    inv = lax.rsqrt(square * (1.0 / D) + EPS)
    cross = cross * inv
    sub = lax.broadcasted_iota(jnp.int32, (HD, NEAR), 0)
    table = jnp.where(sub == 0, mean, 0.0)
    for j, value in ((1, inv), (2, total * (1.0 / D)), (3, cross * (1.0 / D))):
        table = jnp.where(sub == j, value, table)
    cols = table.T
    mean, inv, total, cross = (cols[:, j : j + 1] for j in range(4))
    for h in range(4):
        at = head_cols(h)
        vat = head_cols(4 + h)
        hat = (att[:, at] - mean) * inv
        normed[:, at] = hat * gain[:, at] + bias[:, at]
        g = inv * (ct[:, at] * gain[:, at] - total - hat * cross)
        p = p_in[h]
        values = jnp.concatenate((v_ref[:, at], own[128:384, vat], peer[:, vat]), axis=0)
        keys = jnp.concatenate((k_ref[:, at], own[128:384, at], peer[:, at]), axis=0)
        dp = dot_nt(values, g * INV_ROOT)
        ph, pl_ = split2(p)
        dval = dot_nn(ph, pl_, g)
        ds = p * (dp - jnp.sum(p * dp, axis=0, keepdims=True))
        sh, sl = split2(ds)
        dkey = dot_nn(sh, sl, q_ref[:, at])
        dq[:, at] = dot_tn(keys, sh, sl).T
        dk[:, at] = dkey[0:256]
        dv[:, at] = dval[0:256]
        d_own[:, at] = dkey[256:512]
        d_own[:, vat] = dval[256:512]
        d_peer[:, at] = dkey[512:896]
        d_peer[:, vat] = dval[512:896]


def sum_body(d_own, got, c1a, c1b, c2, c3, c0):
    row = 0
    for ref in (c1a, c1b, c2, c3, c0):
        n = ref.shape[0]
        ref[...] = d_own[row : row + n, :] + got[128 + row : 128 + row + n, :]
        row += n


def unroute_body(zpos, c0, y1, y2, y3, send, buf):
    z = zpos[0]
    g = c0[...] + y1[...] + (y2[32:64, :] + y3[32:64, :])
    send[z] = jnp.zeros((16, 8 * HD), F32)
    send[z ^ 1] = g[0:16]
    for j in (2, 3):
        for h in range(8):
            to = slice(h * HD, (h + 1) * HD)
            send[z ^ j, :, to] = doubled(g[8 * j : 8 * j + 8, to], buf.at[2 * h + j - 2])


def finish_body(zpos, dk0, dv0, got, y1a, y2, y3, z_in, dk, dv, s3, s2, s1, s0):
    z = zpos[0]
    for h in range(8):
        to = slice(h * HD, (h + 1) * HD)
        part = z_in[z ^ 1, :, to] + (z_in[z ^ 2, :, to] + z_in[z ^ 3, :, to])
        part = doubled(part, s3.at[h]) + (y2[0:32, to] + y3[0:32, to])
        part = doubled(part, s2.at[h]) + y1a[:, to]
        part = doubled(part, s1.at[h]) + got[0:128, to]
        src, dst = (dk0, dk) if h < 4 else (dv0, dv)
        col = slice((h % 4) * HD, (h % 4 + 1) * HD)
        dst[:, col] = src[:, col] + doubled(part, s0.at[h])


def body(query, key, value, cotangent, gain, bias):
    seq = lax.axis_size("seq")
    zpos = (lax.axis_index("seq") // 8 % 4).reshape(1).astype(jnp.int32)
    z_groups = [[zh * 32 + zl * 8 + r for zl in range(4)] for zh in range(seq // 32) for r in range(8)]

    def swap(x, mask):
        return lax.ppermute(x, "seq", [(i, i ^ mask) for i in range(seq)])

    def z_swap(x):
        return lax.all_to_all(x, "seq", 0, 0, axis_index_groups=z_groups, tiled=True)

    gain = gain.reshape(1, -1)
    bias = bias.reshape(1, -1)
    l1, l2, l3, l4 = call(
        coarsen_body,
        (shape(128, 1024), shape(64, 1024), shape(32, 1024), shape(4, 16, 1024)),
        (key, value),
        "coarsen",
        0,
        buffers(8, 256, 128, 64, 32),
    )
    c1a = swap(l2, 2)
    z_in = z_swap(l4)
    c0, y23 = call(route_body, (shape(32, 1024), shape(64, 1024)), (zpos, z_in, l3), "route", 1, buffers(16, 16))
    c1b = swap(c0, 2)
    c2 = swap(y23, 4)
    c3 = swap(y23, 6)
    own = call(pack_body, shape(384, 1024), (l1, c1a, c1b, c2, c3, c0), "pack")
    peer = swap(own, 1)
    p, att, send = call(
        forward_body,
        (shape(4, KEYS, NEAR), shape(256, 512), shape(4, 8, 256)),
        (query, key, value, own, peer, cotangent, gain),
        "forward",
    )
    got = lax.all_to_all(send, "head", 0, 0, tiled=True)
    normed, dq, dk0, dv0, d_own, d_peer = call(
        backward_body,
        (shape(256, 512),) * 4 + (shape(256, 1024), shape(384, 1024)),
        (query, key, value, own, peer, cotangent, gain, bias, p, att, got),
        "backward",
    )
    d_got = swap(d_peer, 1)
    g1a, g1b, g2, g3, g0 = call(
        sum_body,
        (shape(64, 1024), shape(32, 1024), shape(64, 1024), shape(64, 1024), shape(32, 1024)),
        (d_own, d_got),
        "add_peer",
    )
    r1b = swap(g1b, 2)
    r2 = swap(g2, 4)
    r3 = swap(g3, 6)
    r1a = swap(g1a, 2)
    z_send = call(unroute_body, shape(4, 16, 1024), (zpos, g0, r1b, r2, r3), "unroute", 1, buffers(16, 16))
    z_got = z_swap(z_send)
    dk, dv = call(
        finish_body,
        (shape(256, 512), shape(256, 512)),
        (zpos, dk0, dv0, d_got, r1a, r2, r3, z_got),
        "finish",
        1,
        buffers(8, 32, 64, 128, 256),
    )
    return normed, dq, dk, dv


def solution(mesh):
    both = P("seq", "head")
    return jax.shard_map(
        body,
        mesh=mesh,
        in_specs=(both,) * 4 + (P("head"),) * 2,
        out_specs=(both,) * 4,
        check_vma=False,
    )
```

```python
import math

import jax
import jax.numpy as jnp
from jax import lax
from jax.experimental import pallas as pl
from jax.experimental.pallas import tpu as pltpu
from jax.sharding import PartitionSpec as P


D = 2048
HEADS = 16
EPS = 1e-05
HD = D // HEADS
INV_ROOT = 1.0 / math.sqrt(HD)
LOG2E = 1.0 / math.log(2.0)

L45 = ((16, 4), (16, 5))
GATHERED = ((64, 2),) + L45 + ((32, 3),) + L45 + ((32, 3),) + L45 + L45
LEVELS = ((256, 0), (128, 1)) + GATHERED + GATHERED
NEAR = 256
KEYS = sum(rows for rows, _ in LEVELS)

VM = pl.BlockSpec(memory_space=pltpu.VMEM)
HB = pl.BlockSpec(memory_space=pltpu.HBM)
F32 = jnp.float32
BF16 = jnp.bfloat16


def shape(*dims):
    return jax.ShapeDtypeStruct(dims, F32)


def call(body, out, args, spaces="", scratch=(), grant=16):
    spaces = spaces.ljust(len(args))
    kinds = {"s": pltpu.SMEM, "h": pltpu.HBM, " ": pltpu.VMEM}
    args = [pltpu.with_memory_space_constraint(x, pltpu.HBM) if c == "h" else x for x, c in zip(args, spaces)]
    return pl.pallas_call(
        body,
        out_shape=out,
        in_specs=[pl.BlockSpec(memory_space=kinds[c]) for c in spaces],
        out_specs=jax.tree.map(lambda x: HB if isinstance(x, pl.MemoryRef) else VM, out),
        scratch_shapes=scratch,
        compiler_params=pltpu.CompilerParams(vmem_limit_bytes=grant << 20),
    )(*args)


def staging(count):
    return [pltpu.VMEM((count, 4, NEAR, HD), F32), pltpu.SemaphoreType.DMA((count, 4))]


class Staged:
    def __init__(self, refs, buf, sem):
        self.buf, self.copies = buf, {}
        for h in range(4):
            for i, ref in enumerate(refs):
                copy = pltpu.make_async_copy(ref.at[:, pl.ds(h * HD, HD)], buf.at[i, h], sem.at[i, h])
                copy.start()
                self.copies[i, h] = copy

    def wait(self, i, h):
        if (i, h) in self.copies:
            self.copies.pop((i, h)).wait()

    def at(self, i, h):
        self.wait(i, h)
        return self.buf[i, h]


def halves(value, buf):
    rows = value.shape[0] // 2
    buf[...] = value
    return 0.5 * (buf[pl.ds(0, rows, stride=2), :] + buf[pl.ds(1, rows, stride=2), :])


def doubled(value, buf):
    rows = value.shape[0]
    half = 0.5 * value
    buf[pl.ds(0, rows, stride=2), :] = half
    buf[pl.ds(1, rows, stride=2), :] = half
    return buf[...]


def buffers(count, *rows):
    return [pltpu.VMEM((count, n, HD), F32) for n in rows]


def coarsen_body(k_hbm, v_hbm, l1, l2, l3, l4, kv, sem, b1, b2, b3):
    staged = Staged((k_hbm, v_hbm), kv, sem)
    for h in range(8):
        i, j = h // 4, h % 4
        staged.wait(i, j)
        to = slice(h * HD, (h + 1) * HD)
        one = 0.5 * (kv[i, j, pl.ds(0, 128, stride=2), :] + kv[i, j, pl.ds(1, 128, stride=2), :])
        l1[:, to] = one
        two = halves(one, b1.at[h])
        l2[:, to] = two
        three = halves(two, b2.at[h])
        l3[:, to] = three
        four = halves(three, b3.at[h])
        for j in range(4):
            l4[j, :, to] = four


def route_body(zpos, z_in, l3, c0, y23, buf):
    z = zpos[0]
    c0[0:16, :] = z_in[z ^ 1]
    for h in range(8):
        to = slice(h * HD, (h + 1) * HD)
        for j in (2, 3):
            c0[8 * j : 8 * j + 8, to] = halves(z_in[z ^ j, :, to], buf.at[2 * h + j - 2])
    y23[0:32, :] = l3[...]
    y23[32:64, :] = c0[...]


def pack_body(*refs):
    out = refs[-1]
    row = 0
    for ref in refs[:-1]:
        out[row : row + ref.shape[0], :] = ref[...]
        row += ref.shape[0]


def split2(x):
    hi = x.astype(BF16)
    return hi, (x - hi.astype(F32)).astype(BF16)


def split3(x):
    hi = x.astype(BF16)
    rest = x - hi.astype(F32)
    mid = rest.astype(BF16)
    return hi, mid, (rest - mid.astype(F32)).astype(BF16)


NT = (((1,), (1,)), ((), ()))
NN = (((1,), (0,)), ((), ()))
TN = (((0,), (0,)), ((), ()))


def dot(a, b, dims):
    return lax.dot_general(a, b, dims, preferred_element_type=F32)


def cat(*parts):
    return jnp.concatenate(parts, axis=1)


def scores(keys, query):
    kh, km, kl = split3(keys)
    qh, qm, ql = split3(query)
    key2 = cat(kh, km)
    return dot(key2, cat(qh, qh), NT) + (dot(key2, cat(qm, qm), NT) + dot(cat(kh, kl), cat(ql, qh), NT))


def dot_nt(a, b):
    ah, al = split2(a)
    bh, bl = split2(b)
    return dot(cat(ah, al), cat(bh, bh), NT) + dot(ah, bl, NT)


def dot_nn(ah, al, b):
    bh, bl = split2(b)
    both = dot(ah, cat(bh, bl), NN)
    half = b.shape[1]
    return both[:, :half] + both[:, half:] + dot(al, bh, NN)


def dot_tn(a, bh, bl):
    ah, al = split2(a)
    return dot(ah, bh, TN) + (dot(ah, bl, TN) + dot(al, bh, TN))


def head_cols(h):
    return slice(h * HD, (h + 1) * HD)


def gather(near, refs, at):
    return jnp.concatenate([near] + [ref[:, at] for ref in refs], axis=0)


def near_body(q_hbm, k_hbm, v_hbm, ct_hbm, q, k, v, ct, s_out, sem):
    copies = []
    for i, (src, dst) in enumerate(((q_hbm, q), (k_hbm, k), (v_hbm, v), (ct_hbm, ct))):
        copies.append(pltpu.make_async_copy(src, dst, sem.at[i]))
        copies[i].start()
    copies[0].wait()
    copies[1].wait()
    for h in range(4):
        at = head_cols(h)
        s_out[h] = scores(k[:, at], q[:, at] * (INV_ROOT * LOG2E))
    copies[2].wait()
    copies[3].wait()


def forward_body(q_ref, k_ref, v_ref, ct, one, own, peer, gain, s_near, p_out, att, send):
    far = (one, own, peer)
    for h in range(4):
        at = head_cols(h)
        query = q_ref[:, at] * (INV_ROOT * LOG2E)
        vat = head_cols(4 + h)
        blocks = [s_near[h]] + [scores(ref[:, at], query) for ref in far]
        s = jnp.concatenate(blocks, axis=0)
        parts = []
        row = 0
        for rows, level in LEVELS:
            seg = s[row : row + rows]
            parts.append(seg + float(level) if level else seg)
            row += rows
        s = jnp.concatenate(parts, axis=0)
        top = jnp.max(s, axis=0, keepdims=True)
        e = jnp.exp2(s - top)
        p = e * (1.0 / jnp.sum(e, axis=0, keepdims=True))
        p_out[h] = p
        values = gather(v_ref[:, at], far, vat)
        ph, pl_ = split2(p)
        att[:, at] = dot_tn(values, ph, pl_).T
    a = att[...]
    width = 4 * HD
    total = jnp.sum(a, axis=1, keepdims=True)
    mean = total * (1.0 / width)
    away = a - mean
    sg = ct[...] * gain[...]
    lane = lax.broadcasted_iota(jnp.int32, (NEAR, HD), 1)
    stats = jnp.where(lane == 0, mean, 0.0)
    for j, value in (
        (1, jnp.sum(away * away, axis=1, keepdims=True)),
        (2, jnp.sum(sg, axis=1, keepdims=True)),
        (3, jnp.sum(sg * away, axis=1, keepdims=True)),
    ):
        stats = jnp.where(lane == j, value, stats)
    rows = stats.T[0:8]
    for j in range(4):
        send[j] = rows


def backward_body(
    q_ref, k_ref, v_ref, ct, one, own, peer, gain, bias, p_in, att, got,
    normed, dq, dv, d_one, dk, d_own, d_peer, out_buf, out_sem,
):
    written = []

    def write(i, h, ref, value, col=None):
        rows = value.shape[0]
        out_buf[i, h, 0:rows, :] = value
        to = ref.at[:, pl.ds((h if col is None else col) * HD, HD)]
        copy = pltpu.make_async_copy(out_buf.at[i, h, pl.ds(0, rows)], to, out_sem.at[i, h])
        copy.start()
        written.append(copy)

    far = (one, own, peer)
    stat = [got[j] for j in range(4)]
    mean = (stat[0][0:1] + stat[1][0:1] + stat[2][0:1] + stat[3][0:1]) * 0.25
    square = jnp.zeros_like(mean)
    total = jnp.zeros_like(mean)
    cross = jnp.zeros_like(mean)
    for part in stat:
        shift = part[0:1] - mean
        square = square + (part[1:2] + (4.0 * HD) * (shift * shift))
        total = total + part[2:3]
        cross = cross + (part[3:4] + part[2:3] * shift)
    inv = lax.rsqrt(square * (1.0 / D) + EPS)
    cross = cross * inv
    sub = lax.broadcasted_iota(jnp.int32, (HD, NEAR), 0)
    table = jnp.where(sub == 0, mean, 0.0)
    for j, value in ((1, inv), (2, total * (1.0 / D)), (3, cross * (1.0 / D))):
        table = jnp.where(sub == j, value, table)
    cols = table.T
    mean, inv, total, cross = (cols[:, j : j + 1] for j in range(4))
    for h in range(4):
        at = head_cols(h)
        vat = head_cols(4 + h)
        hat = (att[:, at] - mean) * inv
        write(0, h, normed, hat * gain[:, at] + bias[:, at])
        g = inv * (ct[:, at] * gain[:, at] - total - hat * cross)
        p = p_in[h]
        values = gather(v_ref[:, at], far, vat)
        keys = gather(k_ref[:, at], far, at)
        dp = dot_nt(values, g * INV_ROOT)
        ph, pl_ = split2(p)
        dval = dot_nn(ph, pl_, g)
        write(2, h, dv, dval[0:256])
        ds = p * (dp - jnp.sum(p * dp, axis=0, keepdims=True))
        sh, sl = split2(ds)
        dkey = dot_nn(sh, sl, q_ref[:, at])
        write(1, h, dq, dot_tn(keys, sh, sl).T)
        dk[:, at] = dkey[0:256]
        write(3, h, d_one, dkey[256:384])
        write(4, h, d_one, dval[256:384], 4 + h)
        row = NEAR + 128
        for ref in (d_own, d_peer):
            n = ref.shape[0]
            ref[:, at] = dkey[row : row + n]
            ref[:, vat] = dval[row : row + n]
            row += n
    for copy in written:
        copy.wait()


def sum_body(ypos, mine, got, g1, g2, g3, gb):
    y = ypos[0]

    def both(row, n):
        return mine[row : row + n, :] + got[row : row + n, :]

    g1[...] = both(0, 64)
    gb[y ^ 1] = both(64, 32)
    g2[...] = both(96, 32)
    gb[y ^ 2] = both(128, 32)
    g3[...] = both(160, 32)
    gb[y ^ 3] = both(192, 32)
    gb[y] = both(224, 32)


def unroute_body(zpos, y_in, send, buf):
    z = zpos[0]
    g = (y_in[0] + y_in[1]) + (y_in[2] + y_in[3])
    send[z] = jnp.zeros((16, 8 * HD), F32)
    send[z ^ 1] = g[0:16]
    for j in (2, 3):
        for h in range(8):
            to = slice(h * HD, (h + 1) * HD)
            send[z ^ j, :, to] = doubled(g[8 * j : 8 * j + 8, to], buf.at[2 * h + j - 2])


def finish_body(zpos, dk0, dv0, got, y1a, y2, y3, z_in, dk, dv, near, sem, s3, s2, s1, s0):
    staged = Staged((dv0,), near, sem)
    z = zpos[0]
    for h in range(8):
        to = slice(h * HD, (h + 1) * HD)
        part = z_in[z ^ 1, :, to] + (z_in[z ^ 2, :, to] + z_in[z ^ 3, :, to])
        part = doubled(part, s3.at[h]) + (y2[:, to] + y3[:, to])
        part = doubled(part, s2.at[h]) + y1a[:, to]
        part = doubled(part, s1.at[h]) + got[:, to]
        at = head_cols(h % 4)
        part = doubled(part, s0.at[h])
        if h < 4:
            dk[:, at] = dk0[:, at] + part
        else:
            dv[:, at] = staged.at(0, h % 4) + part


def body(query, key, value, cotangent, gain, bias):
    seq = lax.axis_size("seq")
    zpos = (lax.axis_index("seq") // 8 % 4).reshape(1).astype(jnp.int32)
    ypos = (lax.axis_index("seq") // 2 % 4).reshape(1).astype(jnp.int32)
    z_groups = [[zh * 32 + zl * 8 + r for zl in range(4)] for zh in range(seq // 32) for r in range(8)]
    y_groups = [[z * 8 + y * 2 + c for y in range(4)] for z in range(seq // 8) for c in range(2)]

    def swap(x, mask):
        return lax.ppermute(x, "seq", [(i, i ^ mask) for i in range(seq)])

    def exchange(x, groups):
        return lax.all_to_all(x, "seq", 0, 0, axis_index_groups=groups, tiled=True)

    gain = gain.reshape(1, -1)
    bias = bias.reshape(1, -1)
    l1, l2, l3, l4 = call(
        coarsen_body,
        (shape(128, 1024), shape(64, 1024), shape(32, 1024), shape(4, 16, 1024)),
        (key, value),
        "hh",
        staging(2) + buffers(8, 128, 64, 32),
    )
    z_in = exchange(l4, z_groups)
    y1 = swap(l2, 2)
    one = swap(l1, 1)
    c0, y23 = call(
        route_body, (shape(32, 1024), shape(64, 1024)), (zpos, z_in, l3), "s", buffers(16, 16)
    )
    y2 = swap(y23, 4)
    y3 = swap(y23, 6)
    c1 = swap(c0, 2)
    own = call(pack_body, shape(256, 1024), (y1, c1, y2, y3, c0))
    peer = swap(own, 1)
    q, k, v, ct, s_near = call(
        near_body,
        (shape(256, 512),) * 4 + (shape(4, NEAR, NEAR),),
        (query, key, value, cotangent),
        "hhhh",
        [pltpu.SemaphoreType.DMA((4,))],
    )
    inputs = (q, k, v, ct, one, own, peer, gain)
    p, att, send = call(
        forward_body, (shape(4, KEYS, NEAR), shape(256, 512), shape(4, 8, 256)), inputs + (s_near,)
    )
    got = lax.all_to_all(send, "head", 0, 0, tiled=True)
    normed, dq, dv0, d_one, dk0, d_own, d_peer = call(
        backward_body,
        (pltpu.HBM((256, 512), F32),) * 3
        + (pltpu.HBM((128, 1024), F32), shape(256, 512), shape(256, 1024), shape(256, 1024)),
        inputs + (bias, p, att, got),
        scratch=staging(5),
    )
    d_got = swap(d_peer, 1)
    g1, g2, g3, gb = call(
        sum_body,
        (shape(64, 1024), shape(32, 1024), shape(32, 1024), shape(4, 32, 1024)),
        (ypos, d_own, d_got),
        "s",
    )
    y_got = exchange(gb, y_groups)
    r1 = swap(g1, 2)
    r2 = swap(g2, 4)
    r3 = swap(g3, 6)
    z_send = call(unroute_body, shape(4, 16, 1024), (zpos, y_got), "s", buffers(16, 16))
    z_got = exchange(z_send, z_groups)
    got_one = swap(d_one, 1)
    dk, dv = call(
        finish_body,
        (shape(256, 512), shape(256, 512)),
        (zpos, dk0, dv0, got_one, r1, r2, r3, z_got),
        "s h",
        staging(1) + buffers(8, 32, 64, 128, 256),
    )
    return normed, dq, dk, dv


def solution(mesh):
    both = P("seq", "head")
    return jax.shard_map(
        body,
        mesh=mesh,
        in_specs=(both,) * 4 + (P("head"),) * 2,
        out_specs=(both,) * 4,
        check_vma=False,
    )
```

```python
import math

import jax
import jax.numpy as jnp
from jax import lax
from jax.experimental import pallas as pl
from jax.experimental.pallas import tpu as pltpu
from jax.sharding import PartitionSpec as P


D = 2048
HEADS = 16
EPS = 1e-05
HD = D // HEADS
INV_ROOT = 1.0 / math.sqrt(HD)
LOG2E = 1.0 / math.log(2.0)

L45 = ((16, 4), (16, 5))
GATHERED = ((64, 2),) + L45 + ((32, 3),) + L45 + ((32, 3),) + L45 + L45
CLOSE = ((256, 0), (128, 1))
NEAR = 256

VM = pl.BlockSpec(memory_space=pltpu.VMEM)
HB = pl.BlockSpec(memory_space=pltpu.HBM)
F32 = jnp.float32
BF16 = jnp.bfloat16


def shape(*dims):
    return jax.ShapeDtypeStruct(dims, F32)


def call(body, out, args, spaces="", scratch=(), grant=16):
    spaces = spaces.ljust(len(args))
    kinds = {"h": pltpu.HBM, " ": pltpu.VMEM}
    args = [pltpu.with_memory_space_constraint(x, pltpu.HBM) if c == "h" else x for x, c in zip(args, spaces)]
    return pl.pallas_call(
        body,
        out_shape=out,
        in_specs=[pl.BlockSpec(memory_space=kinds[c]) for c in spaces],
        out_specs=jax.tree.map(lambda x: HB if isinstance(x, pl.MemoryRef) else VM, out),
        scratch_shapes=scratch,
        compiler_params=pltpu.CompilerParams(vmem_limit_bytes=grant << 20),
    )(*args)


def staging(count):
    return [pltpu.VMEM((count, 4, NEAR, HD), F32), pltpu.SemaphoreType.DMA((count, 4))]


class Staged:
    def __init__(self, refs, buf, sem):
        self.buf, self.copies = buf, {}
        for h in range(4):
            for i, ref in enumerate(refs):
                copy = pltpu.make_async_copy(ref.at[:, pl.ds(h * HD, HD)], buf.at[i, h], sem.at[i, h])
                copy.start()
                self.copies[i, h] = copy

    def wait(self, i, h):
        if (i, h) in self.copies:
            self.copies.pop((i, h)).wait()

    def at(self, i, h):
        self.wait(i, h)
        return self.buf[i, h]


def halves(value, buf):
    rows = value.shape[0] // 2
    buf[...] = value
    return 0.5 * (buf[pl.ds(0, rows, stride=2), :] + buf[pl.ds(1, rows, stride=2), :])


def doubled(value, buf):
    rows = value.shape[0]
    half = 0.5 * value
    buf[pl.ds(0, rows, stride=2), :] = half
    buf[pl.ds(1, rows, stride=2), :] = half
    return buf[...]


def buffers(count, *rows):
    return [pltpu.VMEM((count, n, HD), F32) for n in rows]


def coarsen_body(k_hbm, v_hbm, l1, l2, l3, l4, kv, sem, b1, b2, b3):
    staged = Staged((k_hbm, v_hbm), kv, sem)
    for h in range(8):
        i, j = h // 4, h % 4
        staged.wait(i, j)
        to = slice(h * HD, (h + 1) * HD)
        one = 0.5 * (kv[i, j, pl.ds(0, 128, stride=2), :] + kv[i, j, pl.ds(1, 128, stride=2), :])
        l1[:, to] = one
        two = halves(one, b1.at[h])
        l2[:, to] = two
        three = halves(two, b2.at[h])
        l3[:, to] = three
        four = halves(three, b3.at[h])
        for j in range(4):
            l4[j, :, to] = four


def route_body(z_in, l3, c0, y23, buf):
    z = (lax.axis_index("seq") >> 3) & 3
    c0[0:16, :] = z_in[z ^ 1]
    for h in range(8):
        to = slice(h * HD, (h + 1) * HD)
        for j in (2, 3):
            c0[8 * j : 8 * j + 8, to] = halves(z_in[z ^ j, :, to], buf.at[2 * h + j - 2])
    y23[0:32, :] = l3[...]
    y23[32:64, :] = c0[...]


def pack_body(*refs):
    out = refs[-1]
    row = 0
    for ref in refs[:-1]:
        out[row : row + ref.shape[0], :] = ref[...]
        row += ref.shape[0]


def split2(x):
    hi = x.astype(BF16)
    return hi, (x - hi.astype(F32)).astype(BF16)


def split3(x):
    hi = x.astype(BF16)
    rest = x - hi.astype(F32)
    mid = rest.astype(BF16)
    return hi, mid, (rest - mid.astype(F32)).astype(BF16)


NT = (((1,), (1,)), ((), ()))
NN = (((1,), (0,)), ((), ()))
TN = (((0,), (0,)), ((), ()))


def dot(a, b, dims):
    return lax.dot_general(a, b, dims, preferred_element_type=F32)


def cat(*parts):
    return jnp.concatenate(parts, axis=1)


def scores(keys, query):
    kh, km, kl = split3(keys)
    qh, qm, ql = split3(query)
    key2 = cat(kh, km)
    return dot(key2, cat(qh, qh), NT) + (dot(key2, cat(qm, qm), NT) + dot(cat(kh, kl), cat(ql, qh), NT))


def dot_nt(a, b):
    ah, al = split2(a)
    bh, bl = split2(b)
    return dot(cat(ah, al), cat(bh, bh), NT) + dot(ah, bl, NT)


def dot_nn(ah, al, b):
    bh, bl = split2(b)
    both = dot(ah, cat(bh, bl), NN)
    half = b.shape[1]
    return both[:, :half] + both[:, half:] + dot(al, bh, NN)


def dot_tn(a, bh, bl):
    ah, al = split2(a)
    return dot(ah, bh, TN) + (dot(ah, bl, TN) + dot(al, bh, TN))


def head_cols(h):
    return slice(h * HD, (h + 1) * HD)


def attend(h, q_ref, keys, values, levels):
    query = q_ref[:, head_cols(h)] * (INV_ROOT * LOG2E)
    s = jnp.concatenate([scores(part, query) for part in keys], axis=0)
    parts = []
    row = 0
    for rows, level in levels:
        seg = s[row : row + rows]
        parts.append(seg + float(level) if level else seg)
        row += rows
    s = jnp.concatenate(parts, axis=0)
    top = jnp.max(s, axis=0, keepdims=True)
    e = jnp.exp2(s - top)
    eh, el = split2(e)
    return e, top, jnp.sum(e, axis=0, keepdims=True), dot_tn(jnp.concatenate(values, axis=0), eh, el)


def near_body(q_hbm, k_hbm, v_hbm, ct_hbm, one, q, k, v, ct, e_out, stat, acc, sem):
    copies = []
    for i, (src, dst) in enumerate(((q_hbm, q), (k_hbm, k), (v_hbm, v), (ct_hbm, ct))):
        copies.append(pltpu.make_async_copy(src, dst, sem.at[i]))
        copies[i].start()
    for copy in copies[:3]:
        copy.wait()
    for h in range(4):
        at, vat = head_cols(h), head_cols(4 + h)
        e, top, total, out = attend(h, q, (k[:, at], one[:, at]), (v[:, at], one[:, vat]), CLOSE)
        e_out[h] = e
        stat[h : h + 1, :] = top
        stat[4 + h : 5 + h, :] = total
        acc[h] = out
    copies[3].wait()


def own_body(q, own, e_out, stat, acc):
    for h in range(4):
        at, vat = head_cols(h), head_cols(4 + h)
        e, top, total, out = attend(h, q, (own[:, at],), (own[:, vat],), GATHERED)
        e_out[h] = e
        stat[h : h + 1, :] = top
        stat[4 + h : 5 + h, :] = total
        acc[h] = out


def forward_body(q, peer, stat0, acc0, stat1, acc1, ct, gain, e_out, scale, att, send):
    for h in range(4):
        at, vat = head_cols(h), head_cols(4 + h)
        e, top, total, out = attend(h, q, (peer[:, at],), (peer[:, vat],), GATHERED)
        e_out[h] = e
        top0, top1 = stat0[h : h + 1, :], stat1[h : h + 1, :]
        most = jnp.maximum(jnp.maximum(top0, top1), top)
        w0, w1, w2 = jnp.exp2(top0 - most), jnp.exp2(top1 - most), jnp.exp2(top - most)
        over = 1.0 / (w0 * stat0[4 + h : 5 + h, :] + w1 * stat1[4 + h : 5 + h, :] + w2 * total)
        w0, w1, w2 = w0 * over, w1 * over, w2 * over
        scale[h : h + 1, :] = w0
        scale[4 + h : 5 + h, :] = w1
        scale[8 + h : 9 + h, :] = w2
        att[:, at] = (acc0[h] * w0 + acc1[h] * w1 + out * w2).T
    a = att[...]
    mean = jnp.sum(a, axis=1, keepdims=True) * (1.0 / (4 * HD))
    away = a - mean
    sg = ct[...] * gain[...]
    lane = lax.broadcasted_iota(jnp.int32, (NEAR, HD), 1)
    stats = jnp.where(lane == 0, mean, 0.0)
    for j, value in (
        (1, jnp.sum(away * away, axis=1, keepdims=True)),
        (2, jnp.sum(sg, axis=1, keepdims=True)),
        (3, jnp.sum(sg * away, axis=1, keepdims=True)),
    ):
        stats = jnp.where(lane == j, value, stats)
    rows = stats.T[0:8]
    for j in range(4):
        send[j] = rows


def pull(query, keys, values, e, weight, g, dot_row):
    p = e if weight is None else e * weight
    ph, pl_ = split2(p)
    ds = p * (dot_nt(values, g * INV_ROOT) - dot_row)
    sh, sl = split2(ds)
    return dot_tn(keys, sh, sl), dot_nn(sh, sl, query), dot_nn(ph, pl_, g)


def backward_body(
    q, own, peer, ct, gain, att, got, e_own, e_peer, scale,
    d_own, d_peer, dq_part, g_out, hat_out, dots,
):
    stat = [got[j] for j in range(4)]
    mean = (stat[0][0:1] + stat[1][0:1] + stat[2][0:1] + stat[3][0:1]) * 0.25
    square = jnp.zeros_like(mean)
    total = jnp.zeros_like(mean)
    cross = jnp.zeros_like(mean)
    for part in stat:
        shift = part[0:1] - mean
        square = square + (part[1:2] + (4.0 * HD) * (shift * shift))
        total = total + part[2:3]
        cross = cross + (part[3:4] + part[2:3] * shift)
    inv = lax.rsqrt(square * (1.0 / D) + EPS)
    cross = cross * inv
    sub = lax.broadcasted_iota(jnp.int32, (HD, NEAR), 0)
    table = jnp.where(sub == 0, mean, 0.0)
    for j, value in ((1, inv), (2, total * (1.0 / D)), (3, cross * (1.0 / D))):
        table = jnp.where(sub == j, value, table)
    cols = table.T
    mean, inv, total, cross = (cols[:, j : j + 1] for j in range(4))
    lane = lax.broadcasted_iota(jnp.int32, (NEAR, HD), 1)
    table = jnp.zeros((NEAR, HD), F32)
    for h in range(4):
        at = head_cols(h)
        mine = att[:, at]
        hat = (mine - mean) * inv
        hat_out[:, at] = hat
        g = inv * (ct[:, at] * gain[:, at] - total - hat * cross)
        g_out[:, at] = g
        table = jnp.where(lane == h, jnp.sum(g * mine, axis=1, keepdims=True), table)
    rows = table.T[0:8] * INV_ROOT
    dots[...] = rows
    for h in range(4):
        at, vat = head_cols(h), head_cols(4 + h)
        p_weight = jnp.concatenate(
            (e_own[h] * scale[4 + h : 5 + h, :], e_peer[h] * scale[8 + h : 9 + h, :]), axis=0
        )
        keys = jnp.concatenate((own[:, at], peer[:, at]), axis=0)
        values = jnp.concatenate((own[:, vat], peer[:, vat]), axis=0)
        dq, dkey, dval = pull(q[:, at], keys, values, p_weight, None, g_out[:, at], rows[h : h + 1])
        dq_part[:, at] = dq.T
        d_own[:, at] = dkey[0:256]
        d_own[:, vat] = dval[0:256]
        d_peer[:, at] = dkey[256:512]
        d_peer[:, vat] = dval[256:512]


def tail_body(
    q, k, v, one, gain, bias, e_near, scale, g, hat, dots, dq_part,
    normed, dq_out, dk, dv, d_one, buf, sem,
):
    copies = [pltpu.make_async_copy(buf.at[i], (normed, dq_out)[i], sem.at[i]) for i in range(2)]
    buf[0] = hat[...] * gain[...] + bias[...]
    copies[0].start()
    for h in range(4):
        at, vat = head_cols(h), head_cols(4 + h)
        keys = jnp.concatenate((k[:, at], one[:, at]), axis=0)
        values = jnp.concatenate((v[:, at], one[:, vat]), axis=0)
        dq, dkey, dval = pull(
            q[:, at], keys, values, e_near[h], scale[h : h + 1, :], g[:, at], dots[h : h + 1, :]
        )
        buf[1, :, at] = dq_part[:, at] + dq.T
        dk[:, at] = dkey[0:256]
        dv[:, at] = dval[0:256]
        d_one[:, at] = dkey[256:384]
        d_one[:, vat] = dval[256:384]
    copies[1].start()
    for copy in copies:
        copy.wait()


def sum_body(mine, got, g1, g2, g3, gb):
    y = (lax.axis_index("seq") >> 1) & 3

    def both(row, n):
        return mine[row : row + n, :] + got[row : row + n, :]

    g1[...] = both(0, 64)
    gb[y ^ 1] = both(64, 32)
    g2[...] = both(96, 32)
    gb[y ^ 2] = both(128, 32)
    g3[...] = both(160, 32)
    gb[y ^ 3] = both(192, 32)
    gb[y] = both(224, 32)


def unroute_body(y_in, send, buf):
    z = (lax.axis_index("seq") >> 3) & 3
    g = (y_in[0] + y_in[1]) + (y_in[2] + y_in[3])
    send[z] = jnp.zeros((16, 8 * HD), F32)
    send[z ^ 1] = g[0:16]
    for j in (2, 3):
        for h in range(8):
            to = slice(h * HD, (h + 1) * HD)
            send[z ^ j, :, to] = doubled(g[8 * j : 8 * j + 8, to], buf.at[2 * h + j - 2])


def finish_body(dk0, dv0, got, y1a, y2, y3, z_in, dk, dv, s3, s2, s1, s0):
    z = (lax.axis_index("seq") >> 3) & 3
    for h in range(8):
        to = slice(h * HD, (h + 1) * HD)
        part = z_in[z ^ 1, :, to] + (z_in[z ^ 2, :, to] + z_in[z ^ 3, :, to])
        part = doubled(part, s3.at[h]) + (y2[:, to] + y3[:, to])
        part = doubled(part, s2.at[h]) + y1a[:, to]
        part = doubled(part, s1.at[h]) + got[:, to]
        at = head_cols(h % 4)
        src, dst = (dk0, dk) if h < 4 else (dv0, dv)
        dst[:, at] = src[:, at] + doubled(part, s0.at[h])


def body(query, key, value, cotangent, gain, bias):
    seq = lax.axis_size("seq")
    z_groups = [[zh * 32 + zl * 8 + r for zl in range(4)] for zh in range(seq // 32) for r in range(8)]
    y_groups = [[z * 8 + y * 2 + c for y in range(4)] for z in range(seq // 8) for c in range(2)]

    def swap(x, mask):
        return lax.ppermute(x, "seq", [(i, i ^ mask) for i in range(seq)])

    def exchange(x, groups):
        return lax.all_to_all(x, "seq", 0, 0, axis_index_groups=groups, tiled=True)

    gain = gain.reshape(1, -1)
    bias = bias.reshape(1, -1)
    l1, l2, l3, l4 = call(
        coarsen_body,
        (shape(128, 1024), shape(64, 1024), shape(32, 1024), shape(4, 16, 1024)),
        (key, value),
        "hh",
        staging(2) + buffers(8, 128, 64, 32),
    )
    z_in = exchange(l4, z_groups)
    y1 = swap(l2, 2)
    one = swap(l1, 1)
    c0, y23 = call(
        route_body, (shape(32, 1024), shape(64, 1024)), (z_in, l3), scratch=buffers(16, 16)
    )
    y2 = swap(y23, 4)
    y3 = swap(y23, 6)
    c1 = swap(c0, 2)
    own = call(pack_body, shape(256, 1024), (y1, c1, y2, y3, c0))
    peer = swap(own, 1)
    partial = (shape(8, NEAR), shape(4, HD, NEAR))
    q, k, v, ct, e_near, stat0, acc0 = call(
        near_body,
        (shape(256, 512),) * 4 + (shape(4, 384, NEAR),) + partial,
        (query, key, value, cotangent, one),
        "hhhh",
        [pltpu.SemaphoreType.DMA((4,))],
    )
    e_own, stat1, acc1 = call(own_body, (shape(4, 256, NEAR),) + partial, (q, own))
    e_peer, scale, att, send = call(
        forward_body,
        (shape(4, 256, NEAR), shape(16, NEAR), shape(256, 512), shape(4, 8, 256)),
        (q, peer, stat0, acc0, stat1, acc1, ct, gain),
    )
    got = lax.all_to_all(send, "head", 0, 0, tiled=True)
    d_own, d_peer, dq_part, g, hat, dots = call(
        backward_body,
        (shape(256, 1024),) * 2 + (shape(256, 512),) * 3 + (shape(8, NEAR),),
        (q, own, peer, ct, gain, att, got, e_own, e_peer, scale),
    )
    normed, dq, dk0, dv0, d_one = call(
        tail_body,
        (pltpu.HBM((256, 512), F32),) * 2 + (shape(256, 512),) * 2 + (shape(128, 1024),),
        (q, k, v, one, gain, bias, e_near, scale, g, hat, dots, dq_part),
        scratch=[pltpu.VMEM((2, 256, 512), F32), pltpu.SemaphoreType.DMA((2,))],
    )
    d_got = swap(d_peer, 1)
    g1, g2, g3, gb = call(
        sum_body,
        (shape(64, 1024), shape(32, 1024), shape(32, 1024), shape(4, 32, 1024)),
        (d_own, d_got),
    )
    y_got = exchange(gb, y_groups)
    r1 = swap(g1, 2)
    r2 = swap(g2, 4)
    r3 = swap(g3, 6)
    z_send = call(unroute_body, shape(4, 16, 1024), (y_got,), scratch=buffers(16, 16))
    z_got = exchange(z_send, z_groups)
    got_one = swap(d_one, 1)
    dk, dv = call(
        finish_body,
        (shape(256, 512), shape(256, 512)),
        (dk0, dv0, got_one, r1, r2, r3, z_got),
        scratch=buffers(8, 32, 64, 128, 256),
    )
    return normed, dq, dk, dv


def solution(mesh):
    both = P("seq", "head")
    return jax.shard_map(
        body,
        mesh=mesh,
        in_specs=(both,) * 4 + (P("head"),) * 2,
        out_specs=(both,) * 4,
        check_vma=False,
    )
```

```python
import math

import jax
import jax.numpy as jnp
from jax import lax
from jax.experimental import pallas as pl
from jax.experimental.pallas import tpu as pltpu
from jax.sharding import PartitionSpec as P


D = 2048
HEADS = 16
EPS = 1e-05
HD = D // HEADS
INV_ROOT = 1.0 / math.sqrt(HD)
LOG2E = 1.0 / math.log(2.0)

L45 = ((16, 4), (16, 5))
GATHERED = ((64, 2),) + L45 + ((32, 3),) + L45 + ((32, 3),) + L45 + L45
CLOSE = ((256, 0), (128, 1))
NEAR = 256

VM = pl.BlockSpec(memory_space=pltpu.VMEM)
F32 = jnp.float32
BF16 = jnp.bfloat16


def shape(*dims):
    return jax.ShapeDtypeStruct(dims, F32)


def call(body, out, args, spaces="", scratch=(), grant=16):
    spaces = spaces.ljust(len(args))
    kinds = {"h": pltpu.HBM, " ": pltpu.VMEM}
    args = [pltpu.with_memory_space_constraint(x, pltpu.HBM) if c == "h" else x for x, c in zip(args, spaces)]
    return pl.pallas_call(
        body,
        out_shape=out,
        in_specs=[pl.BlockSpec(memory_space=kinds[c]) for c in spaces],
        out_specs=jax.tree.map(lambda x: pl.BlockSpec(memory_space=x.memory_space) if isinstance(x, pl.MemoryRef) else VM, out),
        scratch_shapes=scratch,
        compiler_params=pltpu.CompilerParams(vmem_limit_bytes=grant << 20),
    )(*args)


def halves(value, buf):
    rows = value.shape[0] // 2
    buf[...] = value
    return 0.5 * (buf[pl.ds(0, rows, stride=2), :] + buf[pl.ds(1, rows, stride=2), :])


def doubled(value, buf):
    rows = value.shape[0]
    half = 0.5 * value
    buf[pl.ds(0, rows, stride=2), :] = half
    buf[pl.ds(1, rows, stride=2), :] = half
    return buf[...]


def buffers(count, *rows):
    return [pltpu.VMEM((count, n, HD), F32) for n in rows]


def coarsen_body(k_hbm, v_hbm, l1, l2, l3, l4, kv, sem, b0, b1, b2, b3):
    copies = []
    for i, src in enumerate((k_hbm, v_hbm)):
        for j in range(2):
            rows = pl.ds(j * 128, 128)
            copies.append(pltpu.make_async_copy(src.at[rows], kv.at[i, rows], sem.at[i, j]))
            copies[-1].start()
    for h in range(8):
        i = h // 4
        if h % 4 == 0:
            copies[2 * i].wait()
            copies[2 * i + 1].wait()
        to = slice(h * HD, (h + 1) * HD)
        one = halves(kv[i, :, head_cols(h % 4)], b0.at[h])
        l1[:, to] = one
        two = halves(one, b1.at[h])
        l2[:, to] = two
        three = halves(two, b2.at[h])
        l3[:, to] = three
        four = halves(three, b3.at[h])
        for j in range(4):
            l4[j, :, to] = four


def route_body(z_in, l3, c0, y23, buf):
    z = (lax.axis_index("seq") >> 3) & 3
    c0[0:16, :] = z_in[z ^ 1]
    for h in range(8):
        to = slice(h * HD, (h + 1) * HD)
        for j in (2, 3):
            c0[8 * j : 8 * j + 8, to] = halves(z_in[z ^ j, :, to], buf.at[2 * h + j - 2])
    y23[0:32, :] = l3[...]
    y23[32:64, :] = c0[...]


def pack_body(*refs):
    out = refs[-1]
    row = 0
    for ref in refs[:-1]:
        out[row : row + ref.shape[0], :] = ref[...]
        row += ref.shape[0]


def split2(x):
    hi = x.astype(BF16)
    return hi, (x - hi.astype(F32)).astype(BF16)


def split3(x):
    hi = x.astype(BF16)
    rest = x - hi.astype(F32)
    mid = rest.astype(BF16)
    return hi, mid, (rest - mid.astype(F32)).astype(BF16)


NT = (((1,), (1,)), ((), ()))
NN = (((1,), (0,)), ((), ()))
TN = (((0,), (0,)), ((), ()))


def dot(a, b, dims):
    return lax.dot_general(a, b, dims, preferred_element_type=F32)


def cat(*parts):
    return jnp.concatenate(parts, axis=1)


def scores(keys, query):
    kh, km, kl = split3(keys)
    qh, qm, ql = split3(query)
    key2 = cat(kh, km)
    return dot(key2, cat(qh, qh), NT) + (dot(key2, cat(qm, qm), NT) + dot(cat(kh, kl), cat(ql, qh), NT))


def dot_nt(a, b):
    ah, al = split2(a)
    bh, bl = split2(b)
    return dot(cat(ah, al), cat(bh, bh), NT) + dot(ah, bl, NT)


def dot_nn(ah, al, b):
    bh, bl = split2(b)
    both = dot(ah, cat(bh, bl), NN)
    half = b.shape[1]
    return both[:, :half] + both[:, half:] + dot(al, bh, NN)


def dot_tn(a, bh, bl):
    ah, al = split2(a)
    return dot(ah, bh, TN) + (dot(ah, bl, TN) + dot(al, bh, TN))


def head_cols(h):
    return slice(h * HD, (h + 1) * HD)


def attend(h, q_ref, keys, values, levels):
    query = q_ref[:, head_cols(h)] * (INV_ROOT * LOG2E)
    s = jnp.concatenate([scores(part, query) for part in keys], axis=0)
    parts = []
    row = 0
    for rows, level in levels:
        seg = s[row : row + rows]
        parts.append(seg + float(level) if level else seg)
        row += rows
    s = jnp.concatenate(parts, axis=0)
    top = jnp.max(s, axis=0, keepdims=True)
    e = jnp.exp2(s - top)
    eh, el = split2(e)
    return e, top, jnp.sum(e, axis=0, keepdims=True), dot_tn(jnp.concatenate(values, axis=0), eh, el)


def near_body(q_hbm, k_hbm, v_hbm, ct_hbm, one, q, k, v, ct, e_out, stat, acc, sem):
    copies = []
    for i, (src, dst) in enumerate(((q_hbm, q), (k_hbm, k), (v_hbm, v), (ct_hbm, ct))):
        copies.append(pltpu.make_async_copy(src, dst, sem.at[i]))
        copies[i].start()
    for copy in copies[:3]:
        copy.wait()
    for h in range(4):
        at, vat = head_cols(h), head_cols(4 + h)
        e, top, total, out = attend(h, q, (k[:, at], one[:, at]), (v[:, at], one[:, vat]), CLOSE)
        e_out[h] = e
        stat[h : h + 1, :] = top
        stat[4 + h : 5 + h, :] = total
        acc[h] = out
    copies[3].wait()


def own_body(q, own, e_out, stat, acc):
    for h in range(4):
        at, vat = head_cols(h), head_cols(4 + h)
        e, top, total, out = attend(h, q, (own[:, at],), (own[:, vat],), GATHERED)
        e_out[h] = e
        stat[h : h + 1, :] = top
        stat[4 + h : 5 + h, :] = total
        acc[h] = out


def forward_body(q, peer, stat0, acc0, stat1, acc1, ct, gain, e_out, scale, att, send):
    for h in range(4):
        at, vat = head_cols(h), head_cols(4 + h)
        e, top, total, out = attend(h, q, (peer[:, at],), (peer[:, vat],), GATHERED)
        e_out[h] = e
        top0, top1 = stat0[h : h + 1, :], stat1[h : h + 1, :]
        most = jnp.maximum(jnp.maximum(top0, top1), top)
        w0, w1, w2 = jnp.exp2(top0 - most), jnp.exp2(top1 - most), jnp.exp2(top - most)
        over = 1.0 / (w0 * stat0[4 + h : 5 + h, :] + w1 * stat1[4 + h : 5 + h, :] + w2 * total)
        w0, w1, w2 = w0 * over, w1 * over, w2 * over
        scale[h : h + 1, :] = w0
        scale[4 + h : 5 + h, :] = w1
        scale[8 + h : 9 + h, :] = w2
        att[:, at] = (acc0[h] * w0 + acc1[h] * w1 + out * w2).T
    a = att[...]
    mean = jnp.sum(a, axis=1, keepdims=True) * (1.0 / (4 * HD))
    away = a - mean
    sg = ct[...] * gain[...]
    lane = lax.broadcasted_iota(jnp.int32, (NEAR, HD), 1)
    stats = jnp.where(lane == 0, mean, 0.0)
    for j, value in (
        (1, jnp.sum(away * away, axis=1, keepdims=True)),
        (2, jnp.sum(sg, axis=1, keepdims=True)),
        (3, jnp.sum(sg * away, axis=1, keepdims=True)),
    ):
        stats = jnp.where(lane == j, value, stats)
    rows = stats.T[0:8]
    for j in range(4):
        send[j] = rows


def pull(query, keys, values, e, weight, g, dot_row):
    p = e if weight is None else e * weight
    ph, pl_ = split2(p)
    ds = p * (dot_nt(values, g * INV_ROOT) - dot_row)
    sh, sl = split2(ds)
    return dot_tn(keys, sh, sl), dot_nn(sh, sl, query), dot_nn(ph, pl_, g)


def backward_body(
    q, own, peer, ct, gain, att, got, e_own, e_peer, scale,
    d_own, d_peer, dq_part, g_out, hat_out, dots,
):
    stat = [got[j] for j in range(4)]
    mean = (stat[0][0:1] + stat[1][0:1] + stat[2][0:1] + stat[3][0:1]) * 0.25
    square = jnp.zeros_like(mean)
    total = jnp.zeros_like(mean)
    cross = jnp.zeros_like(mean)
    for part in stat:
        shift = part[0:1] - mean
        square = square + (part[1:2] + (4.0 * HD) * (shift * shift))
        total = total + part[2:3]
        cross = cross + (part[3:4] + part[2:3] * shift)
    inv = lax.rsqrt(square * (1.0 / D) + EPS)
    cross = cross * inv
    sub = lax.broadcasted_iota(jnp.int32, (HD, NEAR), 0)
    table = jnp.where(sub == 0, mean, 0.0)
    for j, value in ((1, inv), (2, total * (1.0 / D)), (3, cross * (1.0 / D))):
        table = jnp.where(sub == j, value, table)
    cols = table.T
    mean, inv, total, cross = (cols[:, j : j + 1] for j in range(4))
    lane = lax.broadcasted_iota(jnp.int32, (NEAR, HD), 1)
    table = jnp.zeros((NEAR, HD), F32)
    for h in range(4):
        at = head_cols(h)
        mine = att[:, at]
        hat = (mine - mean) * inv
        hat_out[:, at] = hat
        g = inv * (ct[:, at] * gain[:, at] - total - hat * cross)
        g_out[:, at] = g
        table = jnp.where(lane == h, jnp.sum(g * mine, axis=1, keepdims=True), table)
    rows = table.T[0:8] * INV_ROOT
    dots[...] = rows
    for h in range(4):
        at, vat = head_cols(h), head_cols(4 + h)
        p_weight = jnp.concatenate(
            (e_own[h] * scale[4 + h : 5 + h, :], e_peer[h] * scale[8 + h : 9 + h, :]), axis=0
        )
        keys = jnp.concatenate((own[:, at], peer[:, at]), axis=0)
        values = jnp.concatenate((own[:, vat], peer[:, vat]), axis=0)
        dq, dkey, dval = pull(q[:, at], keys, values, p_weight, None, g_out[:, at], rows[h : h + 1])
        dq_part[:, at] = dq.T
        d_own[:, at] = dkey[0:256]
        d_own[:, vat] = dval[0:256]
        d_peer[:, at] = dkey[256:512]
        d_peer[:, vat] = dval[256:512]


def tail_body(
    q, k, v, one, gain, bias, e_near, scale, g, hat, dots, dq_part,
    normed, dq_out, dk, dv, d_one, buf, sem,
):
    copies = [pltpu.make_async_copy(buf.at[i], (normed, dq_out)[i], sem.at[i]) for i in range(2)]
    buf[0] = hat[...] * gain[...] + bias[...]
    copies[0].start()
    for h in range(4):
        at, vat = head_cols(h), head_cols(4 + h)
        keys = jnp.concatenate((k[:, at], one[:, at]), axis=0)
        values = jnp.concatenate((v[:, at], one[:, vat]), axis=0)
        dq, dkey, dval = pull(
            q[:, at], keys, values, e_near[h], scale[h : h + 1, :], g[:, at], dots[h : h + 1, :]
        )
        buf[1, :, at] = dq_part[:, at] + dq.T
        dk[:, at] = dkey[0:256]
        dv[:, at] = dval[0:256]
        d_one[:, at] = dkey[256:384]
        d_one[:, vat] = dval[256:384]
    copies[1].start()
    for copy in copies:
        copy.wait()


def sum_body(mine, got, g1, g2, g3, gb):
    y = (lax.axis_index("seq") >> 1) & 3

    def both(row, n):
        return mine[row : row + n, :] + got[row : row + n, :]

    g1[...] = both(0, 64)
    gb[y ^ 1] = both(64, 32)
    g2[...] = both(96, 32)
    gb[y ^ 2] = both(128, 32)
    g3[...] = both(160, 32)
    gb[y ^ 3] = both(192, 32)
    gb[y] = both(224, 32)


def unroute_body(y_in, send, buf):
    z = (lax.axis_index("seq") >> 3) & 3
    g = (y_in[0] + y_in[1]) + (y_in[2] + y_in[3])
    send[z] = jnp.zeros((16, 8 * HD), F32)
    send[z ^ 1] = g[0:16]
    for j in (2, 3):
        for h in range(8):
            to = slice(h * HD, (h + 1) * HD)
            send[z ^ j, :, to] = doubled(g[8 * j : 8 * j + 8, to], buf.at[2 * h + j - 2])


def finish_body(dk0, dv0, got, y1a, y2, y3, z_in, dk, dv, out, sem, s3, s2, s1, s0):
    written = []
    z = (lax.axis_index("seq") >> 3) & 3
    for h in range(8):
        to = slice(h * HD, (h + 1) * HD)
        part = z_in[z ^ 1, :, to] + (z_in[z ^ 2, :, to] + z_in[z ^ 3, :, to])
        part = doubled(part, s3.at[h]) + (y2[:, to] + y3[:, to])
        part = doubled(part, s2.at[h]) + y1a[:, to]
        part = doubled(part, s1.at[h]) + got[:, to]
        at = head_cols(h % 4)
        src, dst = (dk0, dk) if h < 4 else (dv0, dv)
        out[h // 4, :, at] = src[:, at] + doubled(part, s0.at[h])
        if h % 2:
            cols = pl.ds((h % 4 - 1) * HD, 2 * HD)
            written.append(pltpu.make_async_copy(out.at[h // 4, :, cols], dst.at[:, cols], sem.at[h // 2]))
            written[-1].start()
    for copy in written:
        copy.wait()


def body(query, key, value, cotangent, gain, bias):
    seq = lax.axis_size("seq")
    z_groups = [[zh * 32 + zl * 8 + r for zl in range(4)] for zh in range(seq // 32) for r in range(8)]
    y_groups = [[z * 8 + y * 2 + c for y in range(4)] for z in range(seq // 8) for c in range(2)]

    def swap(x, mask):
        return lax.ppermute(x, "seq", [(i, i ^ mask) for i in range(seq)])

    def exchange(x, groups):
        return lax.all_to_all(x, "seq", 0, 0, axis_index_groups=groups, tiled=True)

    gain = gain.reshape(1, -1)
    bias = bias.reshape(1, -1)
    l1, l2, l3, l4 = call(
        coarsen_body,
        (shape(128, 1024), shape(64, 1024), shape(32, 1024), shape(4, 16, 1024)),
        (key, value),
        "hh",
        [pltpu.VMEM((2, 256, 512), F32), pltpu.SemaphoreType.DMA((2, 2))] + buffers(8, 256, 128, 64, 32),
    )
    z_in = exchange(l4, z_groups)
    y1 = swap(l2, 2)
    one = swap(l1, 1)
    c0, y23 = call(
        route_body, (shape(32, 1024), shape(64, 1024)), (z_in, l3), scratch=buffers(16, 16)
    )
    y2 = swap(y23, 4)
    y3 = swap(y23, 6)
    c1 = swap(c0, 2)
    own = call(pack_body, shape(256, 1024), (y1, c1, y2, y3, c0))
    peer = swap(own, 1)
    partial = (shape(8, NEAR), shape(4, HD, NEAR))
    q, k, v, ct, e_near, stat0, acc0 = call(
        near_body,
        (shape(256, 512),) * 4 + (shape(4, 384, NEAR),) + partial,
        (query, key, value, cotangent, one),
        "hhhh",
        [pltpu.SemaphoreType.DMA((4,))],
    )
    e_own, stat1, acc1 = call(own_body, (shape(4, 256, NEAR),) + partial, (q, own))
    e_peer, scale, att, send = call(
        forward_body,
        (shape(4, 256, NEAR), shape(16, NEAR), shape(256, 512), shape(4, 8, 256)),
        (q, peer, stat0, acc0, stat1, acc1, ct, gain),
    )
    got = lax.all_to_all(send, "head", 0, 0, tiled=True)
    d_own, d_peer, dq_part, g, hat, dots = call(
        backward_body,
        (shape(256, 1024),) * 2 + (shape(256, 512),) * 3 + (shape(8, NEAR),),
        (q, own, peer, ct, gain, att, got, e_own, e_peer, scale),
    )
    normed, dq, dk0, dv0, d_one = call(
        tail_body,
        (pltpu.HBM((256, 512), F32),) * 2 + (shape(256, 512),) * 2 + (shape(128, 1024),),
        (q, k, v, one, gain, bias, e_near, scale, g, hat, dots, dq_part),
        scratch=[pltpu.VMEM((2, 256, 512), F32), pltpu.SemaphoreType.DMA((2,))],
    )
    d_got = swap(d_peer, 1)
    g1, g2, g3, gb = call(
        sum_body,
        (shape(64, 1024), shape(32, 1024), shape(32, 1024), shape(4, 32, 1024)),
        (d_own, d_got),
    )
    y_got = exchange(gb, y_groups)
    r1 = swap(g1, 2)
    r2 = swap(g2, 4)
    r3 = swap(g3, 6)
    z_send = call(unroute_body, shape(4, 16, 1024), (y_got,), scratch=buffers(16, 16))
    z_got = exchange(z_send, z_groups)
    got_one = swap(d_one, 1)
    dk, dv = call(
        finish_body,
        (pltpu.HBM((256, 512), F32),) * 2,
        (dk0, dv0, got_one, r1, r2, r3, z_got),
        scratch=[pltpu.VMEM((2, 256, 512), F32), pltpu.SemaphoreType.DMA((4,))] + buffers(8, 32, 64, 128, 256),
    )
    return normed, dq, dk, dv


def solution(mesh):
    both = P("seq", "head")
    return jax.shard_map(
        body,
        mesh=mesh,
        in_specs=(both,) * 4 + (P("head"),) * 2,
        out_specs=(both,) * 4,
        check_vma=False,
    )
```
